768 devices in a mesh: rep: 32 (over x, y_hi, core), shard: 24 (over y_lo, z).
Axes of the slice: x: 4, y: 8 (y_hi: 4, y_lo: 2; y = y_hi * 2 + y_lo), z: 12, core: 2. Of those that a mesh axis runs over, the one named last changes fastest.
Arguments:
- tokens: bfloat16 [294912, 1536], P(('rep', 'shard')), may hold values from -16 to 16
- patch_mask: int32 [294912], P(('rep', 'shard')), may hold values 0 or 1
- mask_token: bfloat16 [1536], replicated, may hold values from -5 to 5
- student_w: float32 [1536, 768], P('shard'), may hold values from -0.15625 to 0.15625
- teacher_w: float32 [1536, 768], P('shard'), may hold values from -0.15625 to 0.15625
- first_moment: float32 [1536, 768], P('shard'), may hold values from -0.21875 to 0.21875
- second_moment: float32 [1536, 768], P('shard'), may hold values from 2e-05 to 0.0002
Outputs:
- teacher_feat: bfloat16 [294912, 768], P(('rep', 'shard'))
- student_new: float32 [1536, 768], P('shard')
- teacher_new: float32 [1536, 768], P('shard')
- first_new: float32 [1536, 768], P('shard')
- second_new: float32 [1536, 768], P('shard')
- step_direction: float32 [1536, 768], P('shard')
The draws below stay inside these ranges and needn't reach their ends.
All inputs are finite; a program needn't handle non-finite values. No bound on the sum of `patch_mask` on one device may be relied on, other than what follows from the above.
Results may differ from the reference program's by a relative error of at most 0.0049.
Values may be sent and summed in bfloat16 or wider, within the bound.
No kernel may reach another device: no remote copies, remote signals or barrier semaphores. Data moves between devices by JAX's collectives and lax.ppermute only.
A program may use at most 32 MiB of HBM per device.

```python
import math
import jax
import jax.numpy as jnp
from jax import lax

D = 1536
STEP = 100
TOK_DEV = 384
HW = 768
ROWS = 294912


direction_count = 128


spike_factor = 6.0


mixture_scale = 0.015625


def draw_tokens(key, part):
    keys = jax.random.split(jax.random.fold_in(key, 7331), 5)
    blocks = ROWS // TOK_DEV
    block_width = D // blocks
    reach = jax.random.randint(keys[0], (direction_count,), 1, 9)
    coef_raw = jax.random.randint(keys[1], (ROWS, direction_count), -8, 9)
    coef = jnp.clip(coef_raw, -reach[None, :], reach[None, :])
    basis = jax.random.randint(keys[2], (direction_count, D), -3, 4)
    mixture = jnp.dot(coef.astype(jnp.float32), basis.astype(jnp.float32), precision=lax.Precision.HIGHEST) * mixture_scale
    pairing = jax.random.permutation(keys[3], blocks).astype(jnp.int32)
    row_block = (jnp.arange(ROWS) // TOK_DEV).astype(jnp.int32)
    col_block = (jnp.arange(D) // block_width).astype(jnp.int32)
    spiked = pairing[row_block][:, None] == col_block[None, :]
    boost = jnp.where(spiked, spike_factor, 1.0).astype(jnp.float32)
    noise = jax.random.normal(keys[4], (ROWS, D), jnp.float32)
    return jnp.clip(noise * boost + mixture, -16.0, 16.0).astype(jnp.bfloat16)


def touch_ends(array, key, smallest, top_value):
    place = [jax.random.randint(jax.random.fold_in(key, axis), (), 0, length) for axis, length in enumerate(array.shape)]
    main_axis = array.shape.index(max(array.shape))
    neighbour = place[:main_axis] + [(place[main_axis] + 1) % array.shape[main_axis]] + place[main_axis + 1:]
    return array.at[tuple(place)].set(smallest).at[tuple(neighbour)].set(top_value)


def shard_levels(key, dims, pieces, least, largest):
    def one(dim, blocks):
        heights = jax.random.uniform(jax.random.fold_in(jax.random.fold_in(key, 6), dim), (blocks,), jnp.float32, least / len(pieces), largest / len(pieces))
        return jnp.repeat(jnp.exp(heights), dims[dim] // blocks).reshape((-1,) + (1,) * (len(dims) - dim - 1))

    factor_of = one(*pieces[0])
    for cut in pieces[1:]:
        factor_of = factor_of * one(*cut)
    return factor_of


def scatter_about(own_key, dims, scale, most, cuts=(), dtype=jnp.bfloat16):
    result = jax.random.normal(own_key, dims, jnp.float32) * scale
    if len(cuts) > 0:
        result = shard_levels(own_key, dims, cuts, -0.22, 0.18) * result
    return jnp.clip(result, min=-most, max=most).astype(dtype)


def setup_inputs(seed: int = 0) -> dict:
    key_list = jax.random.split(jax.random.key(seed), 8)
    tokens = draw_tokens(jax.random.fold_in(key_list[7], 71), 0)
    patch_mask = touch_ends((jax.random.randint(key_list[1], (ROWS,), 0, 10) < 3).astype(jnp.int32), jax.random.fold_in(key_list[1], 1), 0, 1)
    mask_token = scatter_about(key_list[2], (D,), 0.4, 5.0)
    student_w = scatter_about(key_list[3], (D, HW), D ** -0.5, 0.15625, ((0, 24),), jnp.float32)
    teacher_w = scatter_about(key_list[4], (D, HW), D ** -0.5, 0.15625, ((0, 24),), jnp.float32)
    first_moment = scatter_about(key_list[5], (D, HW), 0.015, 0.21875, ((0, 24),), jnp.float32)
    second_moment = jnp.clip(jnp.exp(math.log(0.0002) - 2.3025851 * jax.random.uniform(key_list[6], (D, HW), jnp.float32) ** shard_levels(key_list[6], (D, HW), ((0, 24),), -0.2, 0.2)), 1.9999999494757503e-05, 0.0002)
    return dict(tokens=tokens, patch_mask=patch_mask, mask_token=mask_token, student_w=student_w, teacher_w=teacher_w, first_moment=first_moment, second_moment=second_moment)


beta_one = 0.9
beta_two = 0.999
adam_eps = 1e-08
learn_rate = 0.0002
decay_rate = 0.04
ema_keep = 0.994

def adamw_update(gradient, weights, teacher, moment_one, moment_two):
    first_new = beta_one * moment_one + (1.0 - beta_one) * gradient
    second_new = beta_two * moment_two + (1.0 - beta_two) * gradient * gradient
    fix_one = 1.0 - beta_one ** STEP
    fix_two = 1.0 - beta_two ** STEP
    direction = first_new / fix_one / (jnp.sqrt(second_new / fix_two) + adam_eps)
    student_new = weights - learn_rate * (direction + decay_rate * weights)
    teacher_new = ema_keep * teacher + (1.0 - ema_keep) * student_new
    return (student_new, teacher_new, first_new, second_new, direction)

def reference(tokens, patch_mask, mask_token, student_w, teacher_w, first_moment, second_moment):
    student_in = jnp.where(patch_mask[:, None] == 1, mask_token[None, :], tokens)
    teacher_feat = jnp.dot(tokens, teacher_w.astype(jnp.bfloat16), preferred_element_type=jnp.float32).astype(jnp.bfloat16)
    student_out = jnp.dot(student_in, student_w.astype(jnp.bfloat16), preferred_element_type=jnp.float32)
    difference = (student_out - teacher_feat.astype(jnp.float32)).astype(jnp.bfloat16)
    gradient = lax.dot_general(student_in, difference, (((0,), (0,)), ((), ())), preferred_element_type=jnp.float32) / ROWS
    student_new, teacher_new, first_new, second_new, direction = adamw_update(gradient, student_w, teacher_w, first_moment, second_moment)
    return (teacher_feat, student_new, teacher_new, first_new, second_new, direction)
```

```python
import jax
import jax.numpy as jnp
from jax import lax
from jax.sharding import Mesh, PartitionSpec as P

STEP = 100


beta_one = 0.9
beta_two = 0.999
adam_eps = 1e-08
learn_rate = 0.0002
decay_rate = 0.04
ema_keep = 0.994

REP = ("x", "yh", "core")
SHARD = ("yl", "z")
SWAP = [(0, 1), (1, 0)]


def adamw_update(gradient, weights, teacher, moment_one, moment_two):
    first_new = beta_one * moment_one + (1.0 - beta_one) * gradient
    second_new = beta_two * moment_two + (1.0 - beta_two) * gradient * gradient
    fix_one = 1.0 - beta_one**STEP
    fix_two = 1.0 - beta_two**STEP
    direction = first_new / fix_one / (jnp.sqrt(second_new / fix_two) + adam_eps)
    student_new = weights - learn_rate * (direction + decay_rate * weights)
    teacher_new = ema_keep * teacher + (1.0 - ema_keep) * student_new
    return (student_new, teacher_new, first_new, second_new, direction)


def spread(piece, axes, members):
    copies = jnp.broadcast_to(piece[None], (members,) + piece.shape)
    return lax.all_to_all(copies, axes, 0, 0, tiled=True)


def exchange(pieces, axes):
    return lax.all_to_all(pieces, axes, 0, 0, tiled=True)


def join_halves(mine, theirs, core):
    return jnp.where(
        core == 0, jnp.concatenate([mine, theirs], 1), jnp.concatenate([theirs, mine], 1)
    )


def shards(tokens, patch_mask, mask_token, student_w, teacher_w, first_moment, second_moment):
    nx, nh, nl, nz = (lax.axis_size(a) for a in ("x", "yh", "yl", "z"))
    shard_count = nl * nz
    core = lax.axis_index("core")
    rows, width = student_w.shape
    half = width // 2
    piece_rows = rows // (nx * nh)
    row_total = float(tokens.shape[0] * shard_count * nx * nh * 2)

    place = (lax.axis_index(("x", "yh")) * piece_rows, core * half)
    cut = lambda w: lax.dynamic_slice(w, place, (piece_rows, half)).astype(jnp.bfloat16)
    piece = jnp.concatenate([cut(student_w), cut(teacher_w)], 1)
    gathered = spread(piece, SHARD, shard_count)
    gathered = lax.all_gather(gathered, "yh", axis=0)
    gathered = gathered.transpose(1, 0, 2, 3).reshape(shard_count, nh * piece_rows, width)
    gathered = spread(gathered, "x", nx)
    weights = gathered.transpose(1, 0, 2, 3).reshape(shard_count * rows, width)

    both = jnp.concatenate([tokens, lax.ppermute(tokens, "core", SWAP)], 0)
    masks = jnp.concatenate([patch_mask, lax.ppermute(patch_mask, "core", SWAP)], 0)
    student_in = jnp.where(masks[:, None] == 1, mask_token[None, :], both)
    teacher_half = jnp.dot(
        both, weights[:, half:], preferred_element_type=jnp.float32
    ).astype(jnp.bfloat16)
    student_out = jnp.dot(student_in, weights[:, :half], preferred_element_type=jnp.float32)
    difference = (student_out - teacher_half.astype(jnp.float32)).astype(jnp.bfloat16)
    local_grad = lax.dot_general(
        student_in, difference, (((0,), (0,)), ((), ())), preferred_element_type=jnp.float32
    )
    own = tokens.shape[0]
    teacher_feat = join_halves(
        teacher_half[:own], lax.ppermute(teacher_half[own:], "core", SWAP), core
    )

    grad = local_grad.astype(jnp.bfloat16).reshape(shard_count, nx, nh * piece_rows, half)
    grad = exchange(grad.transpose(1, 0, 2, 3), "x").astype(jnp.float32).sum(0)
    grad = grad.astype(jnp.bfloat16).reshape(nl, nz, nh, piece_rows, half)
    grad = grad.transpose(2, 0, 1, 3, 4).reshape(nh * nl, nz, piece_rows, half)
    grad = exchange(grad, ("yh", "yl")).astype(jnp.float32).sum(0)
    grad = exchange(grad.astype(jnp.bfloat16), "z").astype(jnp.float32).sum(0)
    grad = join_halves(grad, lax.ppermute(grad, "core", SWAP), core)
    gradient = spread(grad, ("x", "yh"), nx * nh).reshape(rows, width) / row_total
    student_new, teacher_new, first_new, second_new, direction = adamw_update(
        gradient, student_w, teacher_w, first_moment, second_moment
    )
    return (teacher_feat, student_new, teacher_new, first_new, second_new, direction)


def solution(mesh, sizes=(4, 4, 2, 2, 12)):
    fine = Mesh(mesh.devices.reshape(sizes), REP + SHARD)
    tok, row = P(REP + SHARD), P(SHARD, None)
    return jax.shard_map(
        shards,
        mesh=fine,
        in_specs=(P(REP + SHARD, None), tok, P(), row, row, row, row),
        out_specs=(P(REP + SHARD, None), row, row, row, row, row),
        check_vma=False,
    )
```

```python
import jax
import jax.numpy as jnp
from jax import lax
from jax.sharding import Mesh, PartitionSpec as P

STEP = 100


beta_one = 0.9
beta_two = 0.999
adam_eps = 1e-08
learn_rate = 0.0002
decay_rate = 0.04
ema_keep = 0.994

REP = ("x", "yh", "core")
SHARD = ("yl", "z")
SWAP = [(0, 1), (1, 0)]


def adamw_update(gradient, weights, teacher, moment_one, moment_two):
    first_new = beta_one * moment_one + (1.0 - beta_one) * gradient
    second_new = beta_two * moment_two + (1.0 - beta_two) * gradient * gradient
    fix_one = 1.0 - beta_one**STEP
    fix_two = 1.0 - beta_two**STEP
    direction = first_new / fix_one / (jnp.sqrt(second_new / fix_two) + adam_eps)
    student_new = weights - learn_rate * (direction + decay_rate * weights)
    teacher_new = ema_keep * teacher + (1.0 - ema_keep) * student_new
    return (student_new, teacher_new, first_new, second_new, direction)


def spread(piece, axes, members):
    copies = jnp.broadcast_to(piece[None], (members,) + piece.shape)
    return lax.all_to_all(copies, axes, 0, 0, tiled=True)


def exchange(pieces, axes):
    return lax.all_to_all(pieces, axes, 0, 0, tiled=True)


def join_halves(mine, theirs, core):
    return jnp.where(
        core == 0, jnp.concatenate([mine, theirs], 1), jnp.concatenate([theirs, mine], 1)
    )


def shards(tokens, patch_mask, mask_token, student_w, teacher_w, first_moment, second_moment):
    nx, nh, nl, nz = (lax.axis_size(a) for a in ("x", "yh", "yl", "z"))
    shard_count = nl * nz
    core = lax.axis_index("core")
    rows, width = student_w.shape
    half = width // 2
    piece_rows = rows // (nx * nh)
    row_total = float(tokens.shape[0] * shard_count * nx * nh * 2)

    place = (lax.axis_index(("x", "yh")) * piece_rows, core * half)
    cut = lambda w: lax.dynamic_slice(w, place, (piece_rows, half)).astype(jnp.bfloat16)
    piece = jnp.concatenate([cut(student_w), cut(teacher_w)], 1)
    gathered = spread(piece, SHARD, shard_count)

    theirs = lax.ppermute(tokens, "core", SWAP)
    their_mask = lax.ppermute(patch_mask, "core", SWAP)
    gathered, theirs, their_mask = lax.optimization_barrier((gathered, theirs, their_mask))
    both = jnp.concatenate([tokens, theirs], 0)
    masks = jnp.concatenate([patch_mask, their_mask], 0)
    student_in = jnp.where(masks[:, None] == 1, mask_token[None, :], both)

    gathered = lax.all_gather(gathered, "yh", axis=0)
    gathered = gathered.transpose(1, 0, 2, 3).reshape(shard_count, nh * piece_rows, width)
    gathered = spread(gathered, "x", nx).transpose(1, 0, 2, 3)
    student_cols = gathered[..., :half].reshape(shard_count * rows, half)
    teacher_cols = gathered[..., half:].reshape(shard_count * rows, half)

    teacher_half = jnp.dot(both, teacher_cols, preferred_element_type=jnp.float32).astype(
        jnp.bfloat16
    )
    student_out = jnp.dot(student_in, student_cols, preferred_element_type=jnp.float32)
    difference = (student_out - teacher_half.astype(jnp.float32)).astype(jnp.bfloat16)
    local_grad = lax.dot_general(
        student_in, difference, (((0,), (0,)), ((), ())), preferred_element_type=jnp.float32
    )
    own = tokens.shape[0]
    returned = lax.ppermute(teacher_half[own:], "core", SWAP)

    grad = local_grad.astype(jnp.bfloat16).reshape(shard_count, nx, nh * piece_rows, half)
    grad = exchange(grad.transpose(1, 0, 2, 3), "x").astype(jnp.float32).sum(0)
    grad, returned = lax.optimization_barrier((grad, returned))
    teacher_feat = join_halves(teacher_half[:own], returned, core)
    grad = grad.astype(jnp.bfloat16).reshape(nl, nz, nh, piece_rows, half)
    grad = grad.transpose(2, 0, 1, 3, 4).reshape(nh * nl, nz, piece_rows, half)
    grad = exchange(grad, ("yh", "yl")).astype(jnp.float32).sum(0).astype(jnp.bfloat16)
    grad = jnp.broadcast_to(grad[None], (2,) + grad.shape).reshape(2 * nz, piece_rows, half)
    grad = exchange(grad, ("core", "z")).astype(jnp.float32)
    grad = grad.reshape(2, nz, piece_rows, half).sum(1)
    grad = jnp.concatenate([grad[0], grad[1]], 1)
    gradient = spread(grad, ("x", "yh"), nx * nh).reshape(rows, width) / row_total
    student_new, teacher_new, first_new, second_new, direction = adamw_update(
        gradient, student_w, teacher_w, first_moment, second_moment
    )
    return (teacher_feat, student_new, teacher_new, first_new, second_new, direction)


def solution(mesh, sizes=(4, 4, 2, 2, 12)):
    fine = Mesh(mesh.devices.reshape(sizes), REP + SHARD)
    tok, row = P(REP + SHARD), P(SHARD, None)
    return jax.shard_map(
        shards,
        mesh=fine,
        in_specs=(P(REP + SHARD, None), tok, P(), row, row, row, row),
        out_specs=(P(REP + SHARD, None), row, row, row, row, row),
        check_vma=False,
    )
```

```python
import jax
import jax.numpy as jnp
from jax import lax
from jax.sharding import Mesh, PartitionSpec as P

STEP = 100


beta_one = 0.9
beta_two = 0.999
adam_eps = 1e-08
learn_rate = 0.0002
decay_rate = 0.04
ema_keep = 0.994

REP = ("x", "yh", "core")
SHARD = ("yl", "z")
SWAP = [(0, 1), (1, 0)]


def adamw_update(gradient, weights, teacher, moment_one, moment_two):
    first_new = beta_one * moment_one + (1.0 - beta_one) * gradient
    second_new = beta_two * moment_two + (1.0 - beta_two) * gradient * gradient
    fix_one = 1.0 - beta_one**STEP
    fix_two = 1.0 - beta_two**STEP
    direction = first_new / fix_one / (jnp.sqrt(second_new / fix_two) + adam_eps)
    student_new = weights - learn_rate * (direction + decay_rate * weights)
    teacher_new = ema_keep * teacher + (1.0 - ema_keep) * student_new
    return (student_new, teacher_new, first_new, second_new, direction)


def spread(piece, axes, members):
    copies = jnp.broadcast_to(piece[None], (members,) + piece.shape)
    return lax.all_to_all(copies, axes, 0, 0, tiled=True)


def exchange(pieces, axes):
    return lax.all_to_all(pieces, axes, 0, 0, tiled=True)


def halves_in_order(mine, theirs, index):
    return jnp.where(
        index == 0, jnp.concatenate([mine, theirs], 1), jnp.concatenate([theirs, mine], 1)
    )


def shards(tokens, patch_mask, mask_token, student_w, teacher_w, first_moment, second_moment):
    nx, nh, nl, nz = (lax.axis_size(a) for a in ("x", "yh", "yl", "z"))
    core, side = lax.axis_index("core"), lax.axis_index("yl")
    shard_count = nl * nz
    own, depth = tokens.shape
    rows, width = student_w.shape
    half, quarter = width // 2, width // 4
    part = rows // nx
    row_total = float(own * shard_count * nx * nh * 2)

    place = (lax.axis_index("x") * part, core * half)
    cut = lambda w: lax.dynamic_slice(w, place, (part, half)).astype(jnp.bfloat16)
    student_cut, teacher_cut = cut(student_w), cut(teacher_w)
    pieces = jnp.stack(
        [
            jnp.concatenate([student_cut[:, :quarter], teacher_cut[:, :quarter]], 1),
            jnp.concatenate([student_cut[:, quarter:], teacher_cut[:, quarter:]], 1),
        ]
    )
    pieces = jnp.broadcast_to(pieces[:, None], (nl, nz, part, half))
    gathered = exchange(pieces.reshape(shard_count, part, half), SHARD)

    beside = lax.ppermute(tokens, "yl", SWAP)
    beside_mask = lax.ppermute(patch_mask, "yl", SWAP)
    gathered, beside, beside_mask = lax.optimization_barrier((gathered, beside, beside_mask))
    gathered = spread(gathered, "x", nx).transpose(1, 0, 2, 3)
    weights = gathered.reshape(depth, half)

    pair = jnp.concatenate([tokens, beside], 0)
    pair_mask = jnp.concatenate([patch_mask, beside_mask], 0)
    shared = jnp.concatenate([pair, lax.ppermute(pair, "core", SWAP)], 0)
    masks = jnp.concatenate([pair_mask, lax.ppermute(pair_mask, "core", SWAP)], 0)
    masked = masks[:, None] == 1
    student_in = jnp.where(masked, mask_token[None, :], shared)

    product = jnp.dot(shared, weights, preferred_element_type=jnp.float32)
    mask_row = jnp.dot(mask_token[None], weights, preferred_element_type=jnp.float32)
    student_out = jnp.where(masked, mask_row[:, :quarter], product[:, :quarter])
    teacher_part = product[:, quarter:].astype(jnp.bfloat16)
    difference = (student_out - teacher_part.astype(jnp.float32)).astype(jnp.bfloat16)
    local_grad = lax.dot_general(
        student_in, difference, (((0,), (0,)), ((), ())), preferred_element_type=jnp.float32
    )

    grad = local_grad.astype(jnp.bfloat16).reshape(shard_count, nx, part, quarter)
    grad = exchange(grad.transpose(1, 0, 2, 3), "x").astype(jnp.float32).sum(0)

    teacher_part = teacher_part.reshape(2, 2, own, quarter)
    from_side = lax.ppermute(teacher_part[:, 1], "yl", SWAP)
    grad, from_side = lax.optimization_barrier((grad, from_side))
    mine = teacher_part[0, 0]
    to_core = jnp.stack([teacher_part[1, 0], from_side[1]])
    from_core = lax.ppermute(to_core, "core", SWAP)

    grad = exchange(grad.astype(jnp.bfloat16), SHARD).astype(jnp.float32)
    grad = grad.reshape(nl, nz, part, quarter).sum(1)
    grad, from_core = lax.optimization_barrier((grad, from_core))
    teacher_feat = halves_in_order(
        halves_in_order(mine, from_side[0], side),
        halves_in_order(from_core[0], from_core[1], side),
        core,
    )

    grad = jnp.concatenate([grad[0], grad[1]], 1).astype(jnp.bfloat16)
    grad = spread(grad, REP, nx * nh * 2).reshape(nx, nh, 2, part, half)
    grad = grad.astype(jnp.float32).sum(1).transpose(0, 2, 1, 3)
    gradient = grad.reshape(rows, width) / row_total
    student_new, teacher_new, first_new, second_new, direction = adamw_update(
        gradient, student_w, teacher_w, first_moment, second_moment
    )
    return (teacher_feat, student_new, teacher_new, first_new, second_new, direction)


def solution(mesh, sizes=(4, 4, 2, 2, 12)):
    fine = Mesh(mesh.devices.reshape(sizes), REP + SHARD)
    tok, row = P(REP + SHARD), P(SHARD, None)
    return jax.shard_map(
        shards,
        mesh=fine,
        in_specs=(P(REP + SHARD, None), tok, P(), row, row, row, row),
        out_specs=(P(REP + SHARD, None), row, row, row, row, row),
        check_vma=False,
    )
```

```python
import jax
import jax.numpy as jnp
from jax import lax
from jax.experimental import pallas as pl
from jax.experimental.pallas import tpu as pltpu
from jax.sharding import Mesh, PartitionSpec as P


STEP = 100


beta_one = 0.9
beta_two = 0.999
adam_eps = 1e-08
learn_rate = 0.0002
decay_rate = 0.04
ema_keep = 0.994

REP = ("x", "yh", "core")
SHARD = ("yl", "z")
SWAP = [(0, 1), (1, 0)]


def adamw_update(gradient, weights, teacher, moment_one, moment_two):
    first_new = beta_one * moment_one + (1.0 - beta_one) * gradient
    second_new = beta_two * moment_two + (1.0 - beta_two) * gradient * gradient
    fix_one = 1.0 - beta_one**STEP
    fix_two = 1.0 - beta_two**STEP
    direction = first_new / fix_one / (jnp.sqrt(second_new / fix_two) + adam_eps)
    student_new = weights - learn_rate * (direction + decay_rate * weights)
    teacher_new = ema_keep * teacher + (1.0 - ema_keep) * student_new
    return (student_new, teacher_new, first_new, second_new, direction)


def spread(piece, axes, members):
    copies = jnp.broadcast_to(piece[None], (members,) + piece.shape)
    return lax.all_to_all(copies, axes, 0, 0, tiled=True)


def exchange(pieces, axes):
    return lax.all_to_all(pieces, axes, 0, 0, tiled=True)


def halves_in_order(mine, theirs, index):
    return jnp.where(
        index == 0, jnp.concatenate([mine, theirs], 1), jnp.concatenate([theirs, mine], 1)
    )


def products(
    t0, t1, t2, t3, mask_rows, weights, mask_token, features, gradient, blocks, total, sems
):
    own, quarter = features.shape[1:]
    copies = [
        pltpu.make_async_copy(t, blocks.at[j], sems.at[j]) for j, t in enumerate((t0, t1, t2, t3))
    ]
    for copy in copies:
        copy.start()
    by_rows = (((0,), (0,)), ((), ()))
    mask_out = jnp.dot(
        mask_token[...], weights[...], preferred_element_type=jnp.float32
    )[:1, :quarter]
    masked_sum = jnp.zeros((1, quarter), jnp.float32)
    for j, copy in enumerate(copies):
        copy.wait()
        block = blocks[j]
        product = jnp.dot(block, weights[...], preferred_element_type=jnp.float32)
        flags = jnp.broadcast_to(mask_rows[j], (128, own)).T[:, :1] == 1.0
        feature = product[:, quarter:].astype(jnp.bfloat16)
        features[j] = feature
        student = jnp.where(flags, mask_out, product[:, :quarter])
        difference = (student - feature.astype(jnp.float32)).astype(jnp.bfloat16)
        difference = difference.astype(jnp.float32)
        zero = jnp.zeros_like(difference)
        masked_sum += jnp.where(flags, difference, zero).sum(0, keepdims=True)
        kept = jnp.where(flags, zero, difference).astype(jnp.bfloat16)
        part = lax.dot_general(block, kept, by_rows, preferred_element_type=jnp.float32)
        if j == 0:
            total[...] = part
        else:
            total[...] += part
    coarse = masked_sum.astype(jnp.bfloat16).astype(jnp.float32)
    row = lax.broadcasted_iota(jnp.int32, (mask_token.shape[0], quarter), 0)
    terms = jnp.where(row == 0, coarse, jnp.where(row == 1, masked_sum - coarse, 0.0))
    part = lax.dot_general(
        mask_token[...], terms.astype(jnp.bfloat16), by_rows, preferred_element_type=jnp.float32
    )
    full = (total[...] + part).astype(jnp.bfloat16)
    nx, shard_count, rows, _ = gradient.shape
    full = full.reshape(shard_count, nx, rows, quarter)
    for x in range(nx):
        gradient[x] = full[:, x]


def step(tokens, patch_mask, mask_token, student_w, teacher_w, first_moment, second_moment):
    nx, nh, nl, nz = (lax.axis_size(a) for a in ("x", "yh", "yl", "z"))
    core, side = lax.axis_index("core"), lax.axis_index("yl")
    shard_count = nl * nz
    own, depth = tokens.shape
    rows, width = student_w.shape
    half, quarter = width // 2, width // 4
    part = rows // nx
    row_total = float(own * shard_count * nx * nh * 2)

    place = (lax.axis_index("x") * part, core * half)
    cut = lambda w: lax.dynamic_slice(w, place, (part, half)).astype(jnp.bfloat16)
    student_cut, teacher_cut = cut(student_w), cut(teacher_w)
    pieces = jnp.stack(
        [
            jnp.concatenate([student_cut[:, :quarter], teacher_cut[:, :quarter]], 1),
            jnp.concatenate([student_cut[:, quarter:], teacher_cut[:, quarter:]], 1),
        ]
    )
    pieces = jnp.broadcast_to(pieces[:, None], (nl, nz, part, half))
    gathered = exchange(pieces.reshape(shard_count, part, half), SHARD)
    across = lax.ppermute(tokens, "core", SWAP)
    beside = lax.ppermute(tokens, "yl", SWAP)
    gathered, across, beside = lax.optimization_barrier((gathered, across, beside))
    gathered = spread(gathered, "x", nx)
    weights = gathered.transpose(1, 0, 2, 3).reshape(depth, half)
    corner = lax.ppermute(beside, "core", SWAP)
    flags = patch_mask.astype(jnp.float32)
    flags = jnp.stack([flags, lax.ppermute(flags, "yl", SWAP)])
    flags = jnp.concatenate([flags, lax.ppermute(flags, "core", SWAP)])

    any_space = pl.BlockSpec(memory_space=pl.ANY)
    features, grad = pl.pallas_call(
        products,
        in_specs=[any_space] * 4 + [pl.BlockSpec(memory_space=pltpu.VMEM)] * 3,
        out_specs=[pl.BlockSpec(memory_space=pltpu.VMEM)] * 2,
        out_shape=[
            jax.ShapeDtypeStruct((4, own, quarter), jnp.bfloat16),
            jax.ShapeDtypeStruct((nx, shard_count, part, quarter), jnp.bfloat16),
        ],
        scratch_shapes=[
            pltpu.VMEM((4, own, depth), jnp.bfloat16),
            pltpu.VMEM((depth, quarter), jnp.float32),
            pltpu.SemaphoreType.DMA((4,)),
        ],
    )(
        tokens,
        beside,
        across,
        corner,
        flags[:, None, :],
        weights,
        jnp.broadcast_to(mask_token[None], (16, depth)),
    )

    grad = exchange(grad, "x")
    grad = grad.astype(jnp.float32).sum(0)
    from_side = lax.ppermute(features[1::2], "yl", SWAP)
    grad, from_side = lax.optimization_barrier((grad, from_side))
    grad = exchange(grad.astype(jnp.bfloat16), SHARD)
    from_core = lax.ppermute(jnp.stack([features[2], from_side[1]]), "core", SWAP)
    grad, from_core = lax.optimization_barrier((grad, from_core))
    grad = grad.astype(jnp.float32).reshape(nl, nz, part, quarter).sum(1)
    teacher_feat = halves_in_order(
        halves_in_order(features[0], from_side[0], side),
        halves_in_order(from_core[0], from_core[1], side),
        core,
    )

    grad = jnp.concatenate([grad[0], grad[1]], 1).astype(jnp.bfloat16)
    grad = spread(grad, REP, nx * nh * 2)
    grad = grad.reshape(nx, nh, 2, part, half)
    grad = grad.astype(jnp.float32).sum(1).transpose(0, 2, 1, 3)
    gradient = grad.reshape(rows, width) / row_total
    student_new, teacher_new, first_new, second_new, direction = adamw_update(
        gradient, student_w, teacher_w, first_moment, second_moment
    )
    return (teacher_feat, student_new, teacher_new, first_new, second_new, direction)


def solution(mesh, sizes=(4, 4, 2, 2, 12)):
    fine = Mesh(mesh.devices.reshape(sizes), REP + SHARD)
    tok, row = P(REP + SHARD), P(SHARD, None)
    return jax.shard_map(
        step,
        mesh=fine,
        in_specs=(P(REP + SHARD, None), tok, P(), row, row, row, row),
        out_specs=(P(REP + SHARD, None), row, row, row, row, row),
        check_vma=False,
    )
```

```python
import jax
import jax.numpy as jnp
from jax import lax
from jax.experimental import pallas as pl
from jax.experimental.pallas import tpu as pltpu
from jax.sharding import Mesh, PartitionSpec as P


STEP = 100


beta_one = 0.9
beta_two = 0.999
adam_eps = 1e-08
learn_rate = 0.0002
decay_rate = 0.04
ema_keep = 0.994

REP = ("x", "yh", "core")
SHARD = ("yl", "z")
SWAP = [(0, 1), (1, 0)]


def adamw_update(gradient, weights, teacher, moment_one, moment_two):
    first_new = beta_one * moment_one + (1.0 - beta_one) * gradient
    second_new = beta_two * moment_two + (1.0 - beta_two) * gradient * gradient
    fix_one = 1.0 - beta_one**STEP
    fix_two = 1.0 - beta_two**STEP
    direction = first_new / fix_one / (jnp.sqrt(second_new / fix_two) + adam_eps)
    student_new = weights - learn_rate * (direction + decay_rate * weights)
    teacher_new = ema_keep * teacher + (1.0 - ema_keep) * student_new
    return (student_new, teacher_new, first_new, second_new, direction)


def spread(piece, axes, members):
    copies = jnp.broadcast_to(piece[None], (members,) + piece.shape)
    return lax.all_to_all(copies, axes, 0, 0, tiled=True)


def exchange(pieces, axes):
    return lax.all_to_all(pieces, axes, 0, 0, tiled=True)


def halves_in_order(mine, theirs, index):
    return jnp.where(
        index == 0, jnp.concatenate([mine, theirs], 1), jnp.concatenate([theirs, mine], 1)
    )


def products(
    t0, t1, t2, t3, gathered, mask_rows, mask_token, features, gradient, blocks, held, kept, sems
):
    own, quarter = features.shape[1:]
    nx, shard_count, rows, _ = gradient.shape
    loads = [
        pltpu.make_async_copy(gathered.at[x], held.at[:, x], sems.at[x]) for x in range(nx)
    ]
    copies = [
        pltpu.make_async_copy(t, blocks.at[pl.ds(j * own, own)], sems.at[nx + j])
        for j, t in enumerate((t0, t1, t2, t3))
    ]
    for copy in loads + copies:
        copy.start()
    for load in loads:
        load.wait()
    weights = held[...].reshape(nx * shard_count * rows, 2 * quarter)
    mask_out = jnp.dot(mask_token[...], weights, preferred_element_type=jnp.float32)
    mask_out = mask_out[:1, :quarter]
    masked_sum = jnp.zeros((1, quarter), jnp.float32)
    for j, copy in enumerate(copies):
        copy.wait()
        block = blocks[pl.ds(j * own, own)]
        product = jnp.dot(block, weights, preferred_element_type=jnp.float32)
        flags = jnp.broadcast_to(mask_rows[j], (128, own)).T[:, :1] == 1.0
        feature = product[:, quarter:].astype(jnp.bfloat16)
        features[j] = feature
        student = jnp.where(flags, mask_out, product[:, :quarter])
        difference = (student - feature.astype(jnp.float32)).astype(jnp.bfloat16)
        difference = difference.astype(jnp.float32)
        zero = jnp.zeros_like(difference)
        masked_sum += jnp.where(flags, difference, zero).sum(0, keepdims=True)
        kept[pl.ds(j * own, own)] = jnp.where(flags, zero, difference).astype(jnp.bfloat16)
    coarse = masked_sum.astype(jnp.bfloat16).astype(jnp.float32)
    row = lax.broadcasted_iota(jnp.int32, (mask_token.shape[0], quarter), 0)
    terms = jnp.where(row == 0, coarse, jnp.where(row == 1, masked_sum - coarse, 0.0))
    by_rows = (((0,), (0,)), ((), ()))
    total = lax.dot_general(
        blocks[...], kept[...], by_rows, preferred_element_type=jnp.float32
    ) + lax.dot_general(
        mask_token[...], terms.astype(jnp.bfloat16), by_rows, preferred_element_type=jnp.float32
    )
    full = total.astype(jnp.bfloat16).reshape(shard_count, nx, rows, quarter)
    for x in range(nx):
        gradient[x] = full[:, x]


def step(tokens, patch_mask, mask_token, student_w, teacher_w, first_moment, second_moment):
    nx, nh, nl, nz = (lax.axis_size(a) for a in ("x", "yh", "yl", "z"))
    core, side = lax.axis_index("core"), lax.axis_index("yl")
    shard_count = nl * nz
    own, depth = tokens.shape
    rows, width = student_w.shape
    half, quarter = width // 2, width // 4
    part = rows // nx
    row_total = float(own * shard_count * nx * nh * 2)

    place = (lax.axis_index("x") * part, core * half)
    cut = lambda w: lax.dynamic_slice(w, place, (part, half)).astype(jnp.bfloat16)
    student_cut, teacher_cut = cut(student_w), cut(teacher_w)
    pieces = jnp.stack(
        [
            jnp.concatenate([student_cut[:, :quarter], teacher_cut[:, :quarter]], 1),
            jnp.concatenate([student_cut[:, quarter:], teacher_cut[:, quarter:]], 1),
        ]
    )
    pieces = jnp.broadcast_to(pieces[:, None], (nl, nz, part, half))
    gathered = exchange(pieces.reshape(shard_count, part, half), SHARD)
    across = lax.ppermute(tokens, "core", SWAP)
    beside = lax.ppermute(tokens, "yl", SWAP)
    token_rows = jnp.broadcast_to(mask_token[None], (16, depth))
    gathered, across, token_rows = lax.optimization_barrier((gathered, across, token_rows))
    gathered = spread(gathered, "x", nx)
    corner = lax.ppermute(beside, "core", SWAP)
    flags = patch_mask.astype(jnp.float32)
    flags = jnp.stack([flags, lax.ppermute(flags, "yl", SWAP)])
    flags = jnp.concatenate([flags, lax.ppermute(flags, "core", SWAP)])

    any_space = pl.BlockSpec(memory_space=pl.ANY)
    features, grad = pl.pallas_call(
        products,
        in_specs=[any_space] * 5 + [pl.BlockSpec(memory_space=pltpu.VMEM)] * 2,
        out_specs=[pl.BlockSpec(memory_space=pltpu.VMEM)] * 2,
        out_shape=[
            jax.ShapeDtypeStruct((4, own, quarter), jnp.bfloat16),
            jax.ShapeDtypeStruct((nx, shard_count, part, quarter), jnp.bfloat16),
        ],
        scratch_shapes=[
            pltpu.VMEM((4 * own, depth), jnp.bfloat16),
            pltpu.VMEM((shard_count, nx, part, half), jnp.bfloat16),
            pltpu.VMEM((4 * own, quarter), jnp.bfloat16),
            pltpu.SemaphoreType.DMA((nx + 4,)),
        ],
    )(
        tokens,
        beside,
        across,
        corner,
        gathered,
        flags[:, None, :],
        token_rows,
    )

    grad = exchange(grad, "x")
    grad = grad.astype(jnp.float32).sum(0)
    from_side = lax.ppermute(features[1::2], "yl", SWAP)
    grad, from_side = lax.optimization_barrier((grad, from_side))
    grad = exchange(grad.astype(jnp.bfloat16), SHARD)
    from_core = lax.ppermute(jnp.stack([features[2], from_side[1]]), "core", SWAP)
    grad, from_core = lax.optimization_barrier((grad, from_core))
    grad = grad.astype(jnp.float32).reshape(nl, nz, part, quarter).sum(1)
    teacher_feat = halves_in_order(
        halves_in_order(features[0], from_side[0], side),
        halves_in_order(from_core[0], from_core[1], side),
        core,
    )

    grad = jnp.concatenate([grad[0], grad[1]], 1).astype(jnp.bfloat16)
    grad = spread(grad, "yh", nh)
    grad = grad.astype(jnp.float32).sum(0)
    grad = spread(grad, ("x", "core"), nx * 2)
    grad = grad.reshape(nx, 2, part, half).transpose(0, 2, 1, 3)
    gradient = grad.reshape(rows, width) / row_total
    student_new, teacher_new, first_new, second_new, direction = adamw_update(
        gradient, student_w, teacher_w, first_moment, second_moment
    )
    return (teacher_feat, student_new, teacher_new, first_new, second_new, direction)


def solution(mesh, sizes=(4, 4, 2, 2, 12)):
    fine = Mesh(mesh.devices.reshape(sizes), REP + SHARD)
    tok, row = P(REP + SHARD), P(SHARD, None)
    return jax.shard_map(
        step,
        mesh=fine,
        in_specs=(P(REP + SHARD, None), tok, P(), row, row, row, row),
        out_specs=(P(REP + SHARD, None), row, row, row, row, row),
        check_vma=False,
    )
```

```python
import jax
import jax.numpy as jnp
from jax import lax
from jax.experimental import pallas as pl
from jax.experimental.pallas import tpu as pltpu
from jax.sharding import Mesh, PartitionSpec as P


STEP = 100


beta_one = 0.9
beta_two = 0.999
adam_eps = 1e-08
learn_rate = 0.0002
decay_rate = 0.04
ema_keep = 0.994

REP = ("x", "yh", "core")
SHARD = ("yl", "z")
SWAP = [(0, 1), (1, 0)]


def adamw_update(gradient, weights, teacher, moment_one, moment_two):
    first_new = beta_one * moment_one + (1.0 - beta_one) * gradient
    second_new = beta_two * moment_two + (1.0 - beta_two) * gradient * gradient
    fix_one = 1.0 - beta_one**STEP
    fix_two = 1.0 - beta_two**STEP
    direction = first_new / fix_one / (jnp.sqrt(second_new / fix_two) + adam_eps)
    student_new = weights - learn_rate * (direction + decay_rate * weights)
    teacher_new = ema_keep * teacher + (1.0 - ema_keep) * student_new
    return (student_new, teacher_new, first_new, second_new, direction)


def spread(piece, axes, members):
    copies = jnp.broadcast_to(piece[None], (members,) + piece.shape)
    return lax.all_to_all(copies, axes, 0, 0, tiled=True)


def exchange(pieces, axes):
    return lax.all_to_all(pieces, axes, 0, 0, tiled=True)


def halves_in_order(mine, theirs, index):
    return jnp.where(
        index == 0, jnp.concatenate([mine, theirs], 1), jnp.concatenate([theirs, mine], 1)
    )


def products(
    t0, t1, t2, t3, gathered, mask_rows, mask_token, features, gradient, blocks, held, kept, sems
):
    own, quarter = features.shape[1:]
    nx, shard_count, rows, _ = gradient.shape
    loads = [
        pltpu.make_async_copy(gathered.at[x], held.at[:, x], sems.at[x]) for x in range(nx)
    ]
    copies = [
        pltpu.make_async_copy(t, blocks.at[pl.ds(j * own, own)], sems.at[nx + j])
        for j, t in enumerate((t0, t1, t2, t3))
    ]
    for copy in loads + copies:
        copy.start()
    token_rows = jnp.broadcast_to(mask_token[...].astype(jnp.float32), (16, mask_token.shape[1]))
    token_rows = token_rows.astype(jnp.bfloat16)
    for load in loads:
        load.wait()
    weights = held[...].reshape(nx * shard_count * rows, 2 * quarter)
    mask_out = jnp.dot(token_rows, weights, preferred_element_type=jnp.float32)
    mask_out = mask_out[:1, :quarter]
    masked_sum = jnp.zeros((1, quarter), jnp.float32)
    for j, copy in enumerate(copies):
        copy.wait()
        block = blocks[pl.ds(j * own, own)]
        product = jnp.dot(block, weights, preferred_element_type=jnp.float32)
        flags = jnp.broadcast_to(mask_rows[j], (128, own)).T[:, :1] == 1.0
        feature = product[:, quarter:].astype(jnp.bfloat16)
        features[j] = feature
        student = jnp.where(flags, mask_out, product[:, :quarter])
        difference = (student - feature.astype(jnp.float32)).astype(jnp.bfloat16)
        difference = difference.astype(jnp.float32)
        zero = jnp.zeros_like(difference)
        masked_sum += jnp.where(flags, difference, zero).sum(0, keepdims=True)
        kept[pl.ds(j * own, own)] = jnp.where(flags, zero, difference).astype(jnp.bfloat16)
    coarse = masked_sum.astype(jnp.bfloat16).astype(jnp.float32)
    row = lax.broadcasted_iota(jnp.int32, (token_rows.shape[0], quarter), 0)
    terms = jnp.where(row == 0, coarse, jnp.where(row == 1, masked_sum - coarse, 0.0))
    by_rows = (((0,), (0,)), ((), ()))
    total = lax.dot_general(
        blocks[...], kept[...], by_rows, preferred_element_type=jnp.float32
    ) + lax.dot_general(
        token_rows, terms.astype(jnp.bfloat16), by_rows, preferred_element_type=jnp.float32
    )
    full = total.astype(jnp.bfloat16).reshape(shard_count, nx, rows, quarter)
    for x in range(nx):
        gradient[x] = full[:, x]


def step(tokens, patch_mask, mask_token, student_w, teacher_w, first_moment, second_moment):
    nx, nh, nl, nz = (lax.axis_size(a) for a in ("x", "yh", "yl", "z"))
    core, side = lax.axis_index("core"), lax.axis_index("yl")
    shard_count = nl * nz
    own, depth = tokens.shape
    rows, width = student_w.shape
    half, quarter = width // 2, width // 4
    part = rows // nx
    row_total = float(own * shard_count * nx * nh * 2)

    place = (lax.axis_index("x") * part, core * half)
    cut = lambda w: lax.dynamic_slice(w, place, (part, half)).astype(jnp.bfloat16)
    student_cut, teacher_cut = cut(student_w), cut(teacher_w)
    pieces = jnp.stack(
        [
            jnp.concatenate([student_cut[:, :quarter], teacher_cut[:, :quarter]], 1),
            jnp.concatenate([student_cut[:, quarter:], teacher_cut[:, quarter:]], 1),
        ]
    )
    pieces = jnp.broadcast_to(pieces[:, None], (nl, nz, part, half))
    gathered = exchange(pieces.reshape(shard_count, part, half), SHARD)
    across = lax.ppermute(tokens, "core", SWAP)
    beside = lax.ppermute(tokens, "yl", SWAP)
    pair = patch_mask.astype(jnp.float32)
    pair = jnp.stack([pair, lax.ppermute(pair, "core", SWAP)])
    gathered, across, pair = lax.optimization_barrier((gathered, across, pair))
    gathered = spread(gathered, "x", nx)
    corner = lax.ppermute(beside, "core", SWAP)
    flags = jnp.stack([pair, lax.ppermute(pair, "yl", SWAP)], 1).reshape(4, 1, own)

    any_space = pl.BlockSpec(memory_space=pl.ANY)
    features, grad = pl.pallas_call(
        products,
        in_specs=[any_space] * 5 + [pl.BlockSpec(memory_space=pltpu.VMEM)] * 2,
        out_specs=[pl.BlockSpec(memory_space=pltpu.VMEM)] * 2,
        out_shape=[
            jax.ShapeDtypeStruct((4, own, quarter), jnp.bfloat16),
            jax.ShapeDtypeStruct((nx, shard_count, part, quarter), jnp.bfloat16),
        ],
        scratch_shapes=[
            pltpu.VMEM((4 * own, depth), jnp.bfloat16),
            pltpu.VMEM((shard_count, nx, part, half), jnp.bfloat16),
            pltpu.VMEM((4 * own, quarter), jnp.bfloat16),
            pltpu.SemaphoreType.DMA((nx + 4,)),
        ],
    )(
        tokens,
        beside,
        across,
        corner,
        gathered,
        flags,
        mask_token[None],
    )

    grad = exchange(grad, "x")
    grad = grad.astype(jnp.float32).sum(0)
    from_side = lax.ppermute(features[1::2], "yl", SWAP)
    grad, from_side = lax.optimization_barrier((grad, from_side))
    grad = exchange(grad.astype(jnp.bfloat16), SHARD)
    from_core = lax.ppermute(jnp.stack([features[2], from_side[1]]), "core", SWAP)
    grad, from_core = lax.optimization_barrier((grad, from_core))
    grad = grad.astype(jnp.float32).reshape(nl, nz, part, quarter).sum(1)
    teacher_feat = halves_in_order(
        halves_in_order(features[0], from_side[0], side),
        halves_in_order(from_core[0], from_core[1], side),
        core,
    )

    grad = jnp.concatenate([grad[0], grad[1]], 1).astype(jnp.bfloat16)
    grad = spread(grad, "yh", nh)
    grad = grad.astype(jnp.float32).sum(0)
    grad = spread(grad, ("x", "core"), nx * 2)
    grad = grad.reshape(nx, 2, part, half).transpose(0, 2, 1, 3)
    gradient = grad.reshape(rows, width) / row_total
    student_new, teacher_new, first_new, second_new, direction = adamw_update(
        gradient, student_w, teacher_w, first_moment, second_moment
    )
    return (teacher_feat, student_new, teacher_new, first_new, second_new, direction)


def solution(mesh, sizes=(4, 4, 2, 2, 12)):
    fine = Mesh(mesh.devices.reshape(sizes), REP + SHARD)
    tok, row = P(REP + SHARD), P(SHARD, None)
    return jax.shard_map(
        step,
        mesh=fine,
        in_specs=(P(REP + SHARD, None), tok, P(), row, row, row, row),
        out_specs=(P(REP + SHARD, None), row, row, row, row, row),
        check_vma=False,
    )
```

```python
import jax
import jax.numpy as jnp
from jax import lax
from jax.experimental import pallas as pl
from jax.experimental.pallas import tpu as pltpu
from jax.sharding import Mesh, PartitionSpec as P


STEP = 100


beta_one = 0.9
beta_two = 0.999
adam_eps = 1e-08
learn_rate = 0.0002
decay_rate = 0.04
ema_keep = 0.994

REP = ("x", "yh", "core")
SHARD = ("yl", "z")
SWAP = [(0, 1), (1, 0)]


def adamw_update(gradient, weights, teacher, moment_one, moment_two):
    first_new = beta_one * moment_one + (1.0 - beta_one) * gradient
    second_new = beta_two * moment_two + (1.0 - beta_two) * gradient * gradient
    fix_one = 1.0 - beta_one**STEP
    fix_two = 1.0 - beta_two**STEP
    direction = first_new / fix_one / (jnp.sqrt(second_new / fix_two) + adam_eps)
    student_new = weights - learn_rate * (direction + decay_rate * weights)
    teacher_new = ema_keep * teacher + (1.0 - ema_keep) * student_new
    return (student_new, teacher_new, first_new, second_new, direction)


def spread(piece, axes, members):
    copies = jnp.broadcast_to(piece[None], (members,) + piece.shape)
    return lax.all_to_all(copies, axes, 0, 0, tiled=True)


def exchange(pieces, axes):
    return lax.all_to_all(pieces, axes, 0, 0, tiled=True)


def halves_in_order(mine, theirs, index):
    return jnp.where(
        index == 0, jnp.concatenate([mine, theirs], 1), jnp.concatenate([theirs, mine], 1)
    )


def products(
    t0, t1, t2, t3, gathered, mask_rows, mask_token, features, gradient, blocks, held, kept, sems
):
    own, quarter = features.shape[1:]
    nx, shard_count, rows, _ = gathered.shape
    loads = [
        pltpu.make_async_copy(gathered.at[x], held.at[:, x], sems.at[x]) for x in range(nx)
    ]
    copies = [
        pltpu.make_async_copy(t, blocks.at[pl.ds(j * own, own)], sems.at[nx + j])
        for j, t in enumerate((t0, t1, t2, t3))
    ]
    for copy in loads + copies:
        copy.start()
    token_rows = jnp.broadcast_to(mask_token[...].astype(jnp.float32), (16, mask_token.shape[1]))
    token_rows = token_rows.astype(jnp.bfloat16)
    for load in loads:
        load.wait()
    weights = held[...].reshape(nx * shard_count * rows, 2 * quarter)
    mask_out = jnp.dot(token_rows, weights, preferred_element_type=jnp.float32)
    mask_out = mask_out[:1, :quarter]
    masked_sum = jnp.zeros((1, quarter), jnp.float32)
    for j, copy in enumerate(copies):
        copy.wait()
        block = blocks[pl.ds(j * own, own)]
        product = jnp.dot(block, weights, preferred_element_type=jnp.float32)
        flags = jnp.broadcast_to(mask_rows[j], (128, own)).T[:, :1] == 1.0
        feature = product[:, quarter:].astype(jnp.bfloat16)
        features[j] = feature
        student = jnp.where(flags, mask_out, product[:, :quarter])
        difference = (student - feature.astype(jnp.float32)).astype(jnp.bfloat16)
        difference = difference.astype(jnp.float32)
        zero = jnp.zeros_like(difference)
        masked_sum += jnp.where(flags, difference, zero).sum(0, keepdims=True)
        kept[pl.ds(j * own, own)] = jnp.where(flags, zero, difference).astype(jnp.bfloat16)
    coarse = masked_sum.astype(jnp.bfloat16).astype(jnp.float32)
    row = lax.broadcasted_iota(jnp.int32, (token_rows.shape[0], quarter), 0)
    terms = jnp.where(row == 0, coarse, jnp.where(row == 1, masked_sum - coarse, 0.0))
    by_rows = (((0,), (0,)), ((), ()))
    total = lax.dot_general(
        blocks[...], kept[...], by_rows, preferred_element_type=jnp.float32
    ) + lax.dot_general(
        token_rows, terms.astype(jnp.bfloat16), by_rows, preferred_element_type=jnp.float32
    )
    full = total.reshape(shard_count, nx, rows, quarter)
    for x in range(nx):
        paired = jnp.concatenate([full[:, x, : rows // 2], full[:, x, rows // 2 :]], 2)
        gradient[x] = paired.astype(jnp.bfloat16)


def step(tokens, patch_mask, mask_token, student_w, teacher_w, first_moment, second_moment):
    nx, nh, nl, nz = (lax.axis_size(a) for a in ("x", "yh", "yl", "z"))
    core, side = lax.axis_index("core"), lax.axis_index("yl")
    shard_count = nl * nz
    own, depth = tokens.shape
    rows, width = student_w.shape
    half, quarter = width // 2, width // 4
    part = rows // nx
    row_total = float(own * shard_count * nx * nh * 2)

    place = (lax.axis_index("x") * part, core * half)
    cut = lambda w: lax.dynamic_slice(w, place, (part, half)).astype(jnp.bfloat16)
    student_cut, teacher_cut = cut(student_w), cut(teacher_w)
    pieces = jnp.stack(
        [
            jnp.concatenate([student_cut[:, :quarter], teacher_cut[:, :quarter]], 1),
            jnp.concatenate([student_cut[:, quarter:], teacher_cut[:, quarter:]], 1),
        ]
    )
    pieces = jnp.broadcast_to(pieces[:, None], (nl, nz, part, half))
    gathered = exchange(pieces.reshape(shard_count, part, half), SHARD)
    across = lax.ppermute(tokens, "core", SWAP)
    beside = lax.ppermute(tokens, "yl", SWAP)
    pair = patch_mask.astype(jnp.float32)
    pair = jnp.stack([pair, lax.ppermute(pair, "core", SWAP)])
    gathered, across, pair = lax.optimization_barrier((gathered, across, pair))
    gathered = spread(gathered, "x", nx)
    corner = lax.ppermute(beside, "core", SWAP)
    flags = jnp.stack([pair, lax.ppermute(pair, "yl", SWAP)], 1).reshape(4, 1, own)

    any_space = pl.BlockSpec(memory_space=pl.ANY)
    features, grad = pl.pallas_call(
        products,
        in_specs=[any_space] * 5 + [pl.BlockSpec(memory_space=pltpu.VMEM)] * 2,
        out_specs=[pl.BlockSpec(memory_space=pltpu.VMEM)] * 2,
        out_shape=[
            jax.ShapeDtypeStruct((4, own, quarter), jnp.bfloat16),
            jax.ShapeDtypeStruct((nx, shard_count, part // 2, half), jnp.bfloat16),
        ],
        scratch_shapes=[
            pltpu.VMEM((4 * own, depth), jnp.bfloat16),
            pltpu.VMEM((shard_count, nx, part, half), jnp.bfloat16),
            pltpu.VMEM((4 * own, quarter), jnp.bfloat16),
            pltpu.SemaphoreType.DMA((nx + 4,)),
        ],
    )(
        tokens,
        beside,
        across,
        corner,
        gathered,
        flags,
        mask_token[None],
    )

    grad = exchange(grad, "x")
    grad = grad.astype(jnp.float32).sum(0)
    from_side = lax.ppermute(features[1::2], "yl", SWAP)
    grad = exchange(grad.astype(jnp.bfloat16), SHARD)
    from_core = lax.ppermute(jnp.stack([features[2], from_side[1]]), "core", SWAP)
    grad, from_core = lax.optimization_barrier((grad, from_core))
    grad = grad.astype(jnp.float32).reshape(nl, nz, part // 2, half).sum(1)
    grad = jnp.concatenate([grad[..., :quarter], grad[..., quarter:]], 1)
    teacher_feat = halves_in_order(
        halves_in_order(features[0], from_side[0], side),
        halves_in_order(from_core[0], from_core[1], side),
        core,
    )

    grad = jnp.concatenate([grad[0], grad[1]], 1).astype(jnp.bfloat16)
    grad = spread(grad, "yh", nh)
    grad = grad.astype(jnp.float32).sum(0)
    grad = spread(grad, ("x", "core"), nx * 2)
    grad = grad.reshape(nx, 2, part, half).transpose(0, 2, 1, 3)
    gradient = grad.reshape(rows, width) / row_total
    student_new, teacher_new, first_new, second_new, direction = adamw_update(
        gradient, student_w, teacher_w, first_moment, second_moment
    )
    return (teacher_feat, student_new, teacher_new, first_new, second_new, direction)


def solution(mesh, sizes=(4, 4, 2, 2, 12)):
    fine = Mesh(mesh.devices.reshape(sizes), REP + SHARD)
    tok, row = P(REP + SHARD), P(SHARD, None)
    return jax.shard_map(
        step,
        mesh=fine,
        in_specs=(P(REP + SHARD, None), tok, P(), row, row, row, row),
        out_specs=(P(REP + SHARD, None), row, row, row, row, row),
        check_vma=False,
    )
```
